256 devices in a mesh: shift: 8 (over x, core), rows: 32 (over y, z).
Axes of the slice: x: 4, y: 4, z: 8, core: 2. Of those that a mesh axis runs over, the one named last changes fastest.
Arguments:
- neighbours: int32 [256, 8], P('rows'), may hold values from 0 to 255, as said below
- couplings: float32 [256, 8, 128, 128], P('rows'), may hold values from -0.01953125 to 0.01953125
- eigvectors: float32 [256, 128, 128], P('rows'), may hold values from -1 to 1, as said below
- eigvalues: float32 [256, 128], P('rows'), may hold values from -2.5 to 2.5
- start_block: float32 [32768, 128], P('rows'), may hold values from -240 to 240
Outputs:
- basis: float32 [32768, 128], P('rows')
- basis_image: float32 [32768, 128], P('rows')
- projected: float32 [128, 128], replicated
The draws below stay inside these ranges and needn't reach their ends.
Inputs may be any that keep to these rules, and one draw needn't show every extreme that they name: Each block's 8 neighbours are distinct blocks other than itself, each within 8 blocks of it. `eigvectors`: each block's matrix has orthonormal columns up to rounding.
All inputs are finite; a program needn't handle non-finite values.
Results may differ from the reference program's by a relative error of at most 0.00025.
Values sent between devices are 32-bit elements; how exact they have to be, the bound alone decides.
A program may use at most 64 MiB of HBM per device.

```python
import jax
import jax.numpy as jnp
from jax import lax

BLK = 128
NCOL = 128
NNB = 8
SWEEPS = 3
BLK_DEV = 8
NSHIFT = 8
NBLK = 256
NROWS = 32768


def draw_neighbours(key, part):
    offsets = jnp.concatenate([jnp.arange(-BLK_DEV, 0, dtype=jnp.int32), jnp.arange(1, BLK_DEV + 1, dtype=jnp.int32)])
    block_ids = jnp.arange(NBLK, dtype=jnp.int32)[:, None]
    candidates = block_ids + offsets[None, :]
    valid = (candidates >= 0) & (candidates < NBLK)
    scores = jax.random.randint(key, (NBLK, 2 * BLK_DEV), 0, 1 << 20, dtype=jnp.int32)
    scores = scores * (4 * BLK_DEV) + jnp.arange(2 * BLK_DEV, dtype=jnp.int32)[None, :]
    scores = jnp.where(valid, scores, (1 << 30) + jnp.arange(2 * BLK_DEV, dtype=jnp.int32)[None, :])
    order = jnp.argsort(scores, axis=1, stable=True)[:, :NNB]
    return jnp.take_along_axis(candidates, order, axis=1).astype(jnp.int32)


def draw_eigvectors(key, part):
    raw = jax.random.normal(key, (NBLK, BLK, BLK), jnp.float32)
    orthonormal, _ = jnp.linalg.qr(raw)
    return orthonormal.astype(jnp.float32)


def draw_start_block(key, part):
    key_a = jax.random.fold_in(key, 11)
    key_b = jax.random.fold_in(key, 12)
    key_c = jax.random.fold_in(key, 13)
    position = jnp.arange(NROWS, dtype=jnp.float32)[:, None] / NROWS
    rough = jax.random.uniform(key_b, (NROWS, 1), jnp.float32, 0.5, 1.5)
    row_scale = jnp.exp(jnp.log(10.0) * position) * rough
    col_scale = jnp.exp(jnp.log(4.0) * jax.random.uniform(key_c, (1, NCOL), jnp.float32))
    values = jnp.clip(jax.random.normal(key_a, (NROWS, NCOL), jnp.float32), -4.0, 4.0)
    return (values * row_scale * col_scale).astype(jnp.float32)


def steps_of(rng, extent, shards, least, largest):
    def one(dim, blocks):
        draws = jax.random.uniform(jax.random.fold_in(jax.random.fold_in(rng, 6), dim), (blocks,), jnp.float32, least / len(shards), largest / len(shards))
        return jnp.repeat(jnp.exp(draws), extent[dim] // blocks).reshape((-1,) + (1,) * (len(extent) - dim - 1))

    gain = one(*shards[0])
    for cut in shards[1:]:
        gain = gain * one(*cut)
    return gain


def gaussian(rng, extent, spread, bound, shards=(), held_as=jnp.bfloat16):
    gain = steps_of(rng, extent, shards, -0.22, 0.18) if shards else 1.0
    entries = jax.random.normal(rng, extent, jnp.float32) * spread * gain
    return jnp.minimum(jnp.maximum(entries, -bound), bound).astype(held_as)


def setup_inputs(seed: int = 0) -> dict:
    key_of = jax.random.split(jax.random.key(seed), 6)
    return {
        "neighbours": draw_neighbours(jax.random.fold_in(key_of[5], 71), 0),
        "couplings": gaussian(key_of[1], (NBLK, NNB, BLK, BLK), (625 * BLK) ** -0.5, 0.01953125, ((0, 32),), jnp.float32),
        "eigvectors": draw_eigvectors(jax.random.fold_in(key_of[5], 71), 0),
        "eigvalues": jnp.clip(jax.random.uniform(key_of[3], (NBLK, BLK), jnp.float32, -2.5, 2.5) * steps_of(key_of[3], (NBLK, BLK), ((0, 32),), -0.4, 0.0), -2.5, 2.5),
        "start_block": draw_start_block(jax.random.fold_in(key_of[5], 71), 0),
    }


radius = 1.0
damping = 0.8

def unrotate(vectors, field):
    return jnp.einsum('imn,imc->inc', vectors, field, precision=lax.Precision.HIGHEST)

def rotate(vectors, field):
    return jnp.einsum('inm,imc->inc', vectors, field, precision=lax.Precision.HIGHEST)

def shifted_inverse(vectors, values, field, real_part, imag_part):
    width = field.shape[-1] // 2
    spun = unrotate(vectors, field)
    offset = real_part - values
    denom = offset * offset + imag_part * imag_part
    scale_re = (offset / denom)[..., None]
    scale_im = (-imag_part / denom)[..., None]
    first = spun[..., :width]
    second = spun[..., width:]
    mixed = jnp.concatenate([scale_re * first - scale_im * second, scale_re * second + scale_im * first], axis=-1)
    return rotate(vectors, mixed)

def diagonal_part(vectors, values, field):
    return rotate(vectors, values[..., None] * unrotate(vectors, field))

def coupled(near_blocks, couplings):
    return jnp.einsum('iknm,ikmc->inc', couplings, near_blocks, precision=lax.Precision.HIGHEST)

def reference(neighbours, couplings, eigvectors, eigvalues, start_block):
    blocks_b = start_block.reshape(NBLK, BLK, NCOL)
    rhs = jnp.concatenate([blocks_b, jnp.zeros_like(blocks_b)], axis=-1)

    def operate(field):
        return diagonal_part(eigvectors, eigvalues, field) + coupled(field[neighbours], couplings)

    def contour_term(total, index):
        angle = jnp.pi * (index.astype(jnp.float32) + 0.5) / NSHIFT
        real_part = radius * jnp.cos(angle)
        imag_part = radius * jnp.sin(angle)
        iterate = damping * shifted_inverse(eigvectors, eigvalues, rhs, real_part, imag_part)
        for sweep in range(1, SWEEPS):
            first = iterate[..., :NCOL]
            second = iterate[..., NCOL:]
            shifted = jnp.concatenate([real_part * first - imag_part * second, imag_part * first + real_part * second], axis=-1)
            resid = rhs - shifted + operate(iterate)
            iterate = iterate + damping * shifted_inverse(eigvectors, eigvalues, resid, real_part, imag_part)
        term = real_part / NSHIFT * iterate[..., :NCOL] - imag_part / NSHIFT * iterate[..., NCOL:]
        return (total + term, None)
    start = jnp.zeros((NBLK, BLK, NCOL), jnp.float32)
    summed, _ = lax.scan(contour_term, start, jnp.arange(NSHIFT, dtype=jnp.int32))
    field = summed.reshape(NROWS, NCOL)
    gram = jnp.dot(field.T, field, precision=lax.Precision.HIGHEST) / NROWS
    factor = jnp.linalg.cholesky(gram)
    basis = jax.scipy.linalg.solve_triangular(factor, field.T, lower=True).T
    image = operate(basis.reshape(NBLK, BLK, NCOL)).reshape(NROWS, NCOL)
    projected = jnp.dot(basis.T, image, precision=lax.Precision.HIGHEST) / NROWS
    return (basis, image, projected)
```

```python
import functools

import jax
import jax.numpy as jnp
import numpy as np
from jax import lax
from jax.experimental import pallas as pl
from jax.experimental.pallas import tpu as pltpu
from jax.sharding import PartitionSpec as P

MESH = pl.DeviceIdType.MESH
F32 = jnp.float32
BF16 = jnp.bfloat16
BD = 8
N = 128
NN = ((1,), (0,))
NT = ((1,), (1,))
RADIUS = 1.0
DAMPING = 0.8


def split(x):
    hi = x.astype(BF16)
    return hi, (x - hi.astype(F32)).astype(BF16)


def mm(a, b, dims=NN):
    return lax.dot_general(a, b, (dims, ((), ())), preferred_element_type=F32)


def mm3(a, b, dims=NN):
    return mm(a[0], b[0], dims) + (mm(a[0], b[1], dims) + mm(a[1], b[0], dims))


def exact(a, b, dims=NN):
    return lax.dot_general(
        a, b, (dims, ((), ())), precision=lax.Precision.HIGHEST, preferred_element_type=F32
    )


def main_kernel(
    S, R, Z,
    nbr, c_hbm, q_hbm, e_hbm, b_hbm, consts,
    f_out, af_out, g_out,
    cv, c2s, qp, ep, bv, bp, qs, qt, xh, xl, x2, xh2, xl2, y2, dr, di, bt, ft, fh, fa, afs, afa,
    zb, yb, gb,
    csem, qsem, esem, bsem, osem,
    q_s, q_r, qf_s, qf_r, e_s, e_r, b_s, b_r, x_s, x_r, f_s, f_r,
    ga_s, ga_r, gp_s, gp_r, ha_s, ha_r, hp_s, hp_r,
    z_s, z_r, y_s, y_r, g_s, g_r,
):
    W = N // S
    s = lax.axis_index("shift")
    r = lax.axis_index("rows")
    Y = R // Z
    yy, zz = r // Z, r % Z
    core = s % 2
    partner = s + 1 - 2 * core
    up, down = (r + 1) % R, (r + R - 1) % R
    X = S // 2
    xx = s // 2

    load_q = pltpu.make_async_copy(q_hbm, qp.at[pl.ds(BD, BD)], qsem)
    load_q.start()
    load_b = pltpu.make_async_copy(b_hbm, bv, bsem)
    load_b.start()
    load_e = pltpu.make_async_copy(e_hbm, ep.at[1], esem)
    load_e.start()
    load_c = pltpu.make_async_copy(c_hbm, cv, csem)
    load_c.start()

    barrier = pltpu.get_barrier_semaphore()

    def greet(where):
        pl.semaphore_signal(barrier, inc=1, device_id=where, device_id_type=MESH)

    greet({"rows": up})
    greet({"rows": down})
    for k in range(1, Z):
        greet({"rows": yy * Z + (zz + k) % Z})
    for k in range(1, Y):
        greet({"rows": ((yy + k) % Y) * Z + zz})
    for k in range(1, S):
        greet({"shift": (s + k) % S})
    pl.semaphore_wait(barrier, 2 + (Z - 1) + (Y - 1) + (S - 1))

    def remote(src, dst, ss, rs, where):
        return pltpu.make_async_remote_copy(
            src_ref=src, dst_ref=dst, send_sem=ss, recv_sem=rs,
            device_id=where, device_id_type=MESH,
        )

    HB = BD // 2
    q_up = remote(q_hbm.at[pl.ds(core * HB, HB)], qp.at[pl.ds(core * HB, HB)],
                  q_s.at[0], q_r.at[0], {"rows": up})
    q_dn = remote(q_hbm.at[pl.ds(core * HB, HB)], qp.at[pl.ds(2 * BD + core * HB, HB)],
                  q_s.at[1], q_r.at[1], {"rows": down})
    q_up.start()
    q_dn.start()
    e_up = remote(e_hbm, ep.at[0], e_s.at[0], e_r.at[0], {"rows": up})
    e_dn = remote(e_hbm, ep.at[2], e_s.at[1], e_r.at[1], {"rows": down})
    e_up.start()
    e_dn.start()

    lane = lax.broadcasted_iota(jnp.int32, (W, N), 1)
    row = lax.broadcasted_iota(jnp.int32, (W, N), 0)
    pick = (lane == row + s * W).astype(BF16)
    fold = (lane % W == row).astype(BF16)

    load_q.wait()
    load_b.wait()
    load_e.wait()

    def own_rhs(i, _):
        q = qp[BD + i]
        qh, ql = split(q)
        qs[0, i] = qh
        qs[1, i] = ql
        th, tl = split(q.T)
        qt[0, i] = th
        qt[1, i] = tl
        blk = bv[pl.ds(pl.multiple_of(i * N, N), N), :]
        bh = blk.astype(BF16)
        rest = blk - bh.astype(F32)
        bl = rest.astype(BF16)
        bm = (rest - bl.astype(F32)).astype(BF16)
        own = mm(pick, bh, NT) + (mm(pick, bl, NT) + mm(pick, bm, NT))
        bp[BD + i] = mm3(split(own), (qh, ql))
        return 0

    lax.fori_loop(0, BD, own_rhs, 0)

    b_up = remote(bp.at[pl.ds(BD, BD)], bp.at[pl.ds(0, BD)], b_s.at[0], b_r.at[0], {"rows": up})
    b_dn = remote(bp.at[pl.ds(BD, BD)], bp.at[pl.ds(2 * BD, BD)], b_s.at[1], b_r.at[1], {"rows": down})
    b_up.start()
    b_dn.start()

    za = consts[0:1, :]
    zbm = consts[1:2, :]
    wr = consts[2:3, :]
    wi = consts[3:4, :]

    def coefficients(e_row):
        offset = za - jnp.broadcast_to(e_row, (N, N)).T
        scale = DAMPING / (offset * offset + zbm * zbm)
        return offset * scale, -zbm * scale

    def spread(rhs):
        return jnp.concatenate([rhs] * S, axis=0).T

    def first(g, slot, qpair):
        c_re, c_im = coefficients(g)
        tile = spread(bp[slot])
        mixed = jnp.concatenate([c_re * tile, c_im * tile], axis=1)
        xv = mm3(qpair, split(mixed))
        h, l = split(xv)
        xh[slot] = h
        xl[slot] = l
        return c_re, c_im, tile, mixed

    def own_first(i, _):
        c_re, c_im, tile, mixed = first(ep[1, pl.ds(i, 1), :], BD + i, (qs[0, i], qs[1, i]))
        dr[i] = c_re
        di[i] = c_im
        bt[i] = tile
        y2[i] = mixed
        return 0

    lax.fori_loop(0, BD, own_first, 0)

    load_c.wait()

    def split_c(i, _):
        for k in range(BD):
            h, l = split(cv[i, k])
            c2s[i, 0:N, k * N:(k + 1) * N] = h
            c2s[i, N:2 * N, k * N:(k + 1) * N] = l
        return 0

    lax.fori_loop(0, BD, split_c, 0)

    q_up.wait_recv()
    qf_lo = remote(qp.at[pl.ds(core * HB, HB)], qp.at[pl.ds(core * HB, HB)],
                   qf_s.at[0], qf_r.at[0], {"shift": partner})
    qf_lo.start()
    q_dn.wait_recv()
    qf_hi = remote(qp.at[pl.ds(2 * BD + core * HB, HB)], qp.at[pl.ds(2 * BD + core * HB, HB)],
                   qf_s.at[1], qf_r.at[1], {"shift": partner})
    qf_hi.start()
    e_up.wait_recv()
    e_dn.wait_recv()
    b_up.wait_recv()
    b_dn.wait_recv()
    qf_lo.wait_recv()
    qf_hi.wait_recv()

    def halo_first(i, _):
        first(ep[0, pl.ds(i, 1), :], i, split(qp[i]))
        first(ep[2, pl.ds(i, 1), :], 2 * BD + i, split(qp[2 * BD + i]))
        return 0

    lax.fori_loop(0, BD, halo_first, 0)

    base = r * BD - BD

    def place(i, k):
        return jnp.clip(nbr[i, k] - base, 0, 3 * BD - 1)

    def coupled(i, hi_ref, lo_ref):
        acc = jnp.zeros((N, 2 * N), F32)
        for k in range(0, BD, 2):
            i0 = place(i, k)
            i1 = place(i, k + 1)
            hi = jnp.concatenate([hi_ref[i0], hi_ref[i1]], axis=0)
            lo = jnp.concatenate([lo_ref[i0], lo_ref[i1]], axis=0)
            both = mm(c2s[i, :, k * N:(k + 2) * N], hi)
            acc = acc + both[:N] + both[N:] + mm(c2s[i, :N, k * N:(k + 2) * N], lo)
        return acc

    def relaxed(i, hi_ref, lo_ref):
        spun = mm3((qt[0, i], qt[1, i]), split(coupled(i, hi_ref, lo_ref)))
        t_re = bt[i] + spun[:, :N]
        t_im = spun[:, N:]
        c_re, c_im = dr[i], di[i]
        old = y2[i]
        return (
            (1.0 - DAMPING) * old[:, :N] + (c_re * t_re - c_im * t_im),
            (1.0 - DAMPING) * old[:, N:] + (c_re * t_im + c_im * t_re),
        )

    def x_copies(i):
        return (
            remote(x2.at[BD + i], x2.at[i], x_s.at[0, i], x_r.at[0, i], {"rows": up}),
            remote(x2.at[BD + i], x2.at[2 * BD + i], x_s.at[1, i], x_r.at[1, i], {"rows": down}),
        )

    def sweep_one(i, _):
        re, im = relaxed(i, xh, xl)
        mixed = jnp.concatenate([re, im], axis=1)
        y2[i] = mixed
        xv = mm3((qs[0, i], qs[1, i]), split(mixed))
        x2[BD + i] = xv
        to_up, to_dn = x_copies(i)
        to_up.start()
        to_dn.start()
        h, l = split(xv)
        xh2[BD + i] = h
        xl2[BD + i] = l
        return 0

    lax.fori_loop(0, BD, sweep_one, 0)

    def arrive(i, _):
        to_up, to_dn = x_copies(i)
        to_up.wait_recv()
        h, l = split(x2[i])
        xh2[i] = h
        xl2[i] = l
        to_dn.wait_recv()
        h, l = split(x2[2 * BD + i])
        xh2[2 * BD + i] = h
        xl2[2 * BD + i] = l
        return 0

    lax.fori_loop(0, BD, arrive, 0)

    def sweep_two(i, _):
        re, im = relaxed(i, xh2, xl2)
        t = wr * re - wi * im
        t0 = t.astype(BF16)
        rest = t - t0.astype(F32)
        t1 = rest.astype(BF16)
        t2 = (rest - t1.astype(F32)).astype(BF16)
        hat = mm(fold, t0, NT) + (mm(fold, t1, NT) + mm(fold, t2, NT))
        fh[i] = hat
        ft[BD + i] = mm3(split(hat), (qs[0, i], qs[1, i]), NT)
        return 0

    lax.fori_loop(0, BD, sweep_two, 0)

    f_up = remote(ft.at[pl.ds(BD, BD)], ft.at[pl.ds(0, BD)], f_s.at[0], f_r.at[0], {"rows": up})
    f_dn = remote(ft.at[pl.ds(BD, BD)], ft.at[pl.ds(2 * BD, BD)], f_s.at[1], f_r.at[1], {"rows": down})
    f_up.start()
    f_dn.start()

    def gather_start(src, dst, ssem, rsem, psem, prsem):
        cross = []
        for k in range(1, X):
            c = remote(src, dst.at[s], ssem.at[k], rsem.at[k], {"shift": ((xx + k) % X) * 2 + core})
            c.start()
            cross.append(c)
        mine = remote(src, dst.at[s], psem.at[0], prsem.at[0], {"shift": partner})
        mine.start()
        return cross, mine

    def gather_forward(dst, cross, psem, prsem):
        on = []
        for k in range(1, X):
            cross[k - 1].wait_recv()
            origin = ((xx + X - k) % X) * 2 + core
            c = remote(dst.at[origin], dst.at[origin], psem.at[k], prsem.at[k], {"shift": partner})
            c.start()
            on.append(c)
        return on

    def gather_end(mine, on):
        mine.wait_recv()
        for c in on:
            c.wait_recv()

    f_cross, f_mine = gather_start(ft.at[pl.ds(BD, BD)], fa, ga_s, ga_r, gp_s, gp_r)
    fa[s] = ft[pl.ds(BD, BD)]
    f_up.wait_recv()
    f_dn.wait_recv()

    def image(i, _):
        acc = mm3(split(fh[i] * ep[1, pl.ds(i, 1), :]), (qs[0, i], qs[1, i]), NT)
        for k in range(0, BD, 2):
            i0 = place(i, k)
            i1 = place(i, k + 1)
            near = jnp.concatenate([ft[i0], ft[i1]], axis=1)
            h, l = split(near)
            ch = c2s[i, :N, k * N:(k + 2) * N]
            cl = c2s[i, N:, k * N:(k + 2) * N]
            acc = acc + mm3((h, l), (ch, cl), NT)
        afs[i] = acc
        return 0

    lax.fori_loop(0, BD, image, 0)

    f_on = gather_forward(fa, f_cross, gp_s, gp_r)
    h_cross, h_mine = gather_start(afs, afa, ha_s, ha_r, hp_s, hp_r)
    afa[s] = afs[...]
    gather_end(f_mine, f_on)
    out_f = pltpu.make_async_copy(fa, f_out, osem.at[0])
    out_f.start()

    def grams(i, acc):
        left = jnp.concatenate([ft[BD + i], afs[i]], axis=0)
        right = jnp.concatenate([fa[t, i] for t in range(S)], axis=0)
        return acc + exact(left, right, NT)

    zb[zz] = lax.fori_loop(0, BD, grams, jnp.zeros((2 * W, N), F32))

    z_cp = []
    for k in range(1, Z):
        c = remote(zb.at[zz], zb.at[zz], z_s.at[k], z_r.at[k], {"rows": yy * Z + (zz + k) % Z})
        c.start()
        z_cp.append(c)
    h_on = gather_forward(afa, h_cross, hp_s, hp_r)
    for c in z_cp:
        c.wait_recv()
    yb[yy] = functools.reduce(lambda a, t: a + zb[t], range(1, Z), zb[0])
    y_cp = []
    for k in range(1, Y):
        c = remote(yb.at[yy], yb.at[yy], y_s.at[k], y_r.at[k], {"rows": ((yy + k) % Y) * Z + zz})
        c.start()
        y_cp.append(c)
    for c in y_cp:
        c.wait_recv()
    gb[s] = functools.reduce(lambda a, t: a + yb[t], range(1, Y), yb[0])
    g_cp = []
    for k in range(1, S):
        c = remote(gb.at[s], gb.at[s], g_s.at[k], g_r.at[k], {"shift": (s + k) % S})
        c.start()
        g_cp.append(c)
    gather_end(h_mine, h_on)
    out_h = pltpu.make_async_copy(afa, af_out, osem.at[1])
    out_h.start()
    for c in g_cp:
        c.wait_recv()
    out_g = pltpu.make_async_copy(gb, g_out, osem.at[2])
    out_g.start()

    for c in (q_up, q_dn, e_up, e_dn, b_up, b_dn, qf_lo, qf_hi, f_up, f_dn):
        c.wait_send()
    for c in f_cross + [f_mine] + f_on + h_cross + [h_mine] + h_on + z_cp + y_cp + g_cp:
        c.wait_send()

    def sent(i, _):
        to_up, to_dn = x_copies(i)
        to_up.wait_send()
        to_dn.wait_send()
        return 0

    lax.fori_loop(0, BD, sent, 0)
    out_f.wait()
    out_h.wait()
    out_g.wait()


def inverse_factor(g):
    T, B = N // 8, 32
    sub = lax.broadcasted_iota(jnp.int32, (8, N), 0)
    lane = lax.broadcasted_iota(jnp.int32, (8, N), 1)
    a = [g[8 * t:8 * t + 8] for t in range(T)]
    m = [(lane == sub + 8 * t).astype(F32) for t in range(T)]
    for p in range(N // B):
        last = (p + 1) * B // 8
        for k in range(p * B, (p + 1) * B):
            t0, r0 = k // 8, k % 8
            head = jnp.broadcast_to(a[t0][:, k:k + 1], (8, N))
            inv = lax.rsqrt(jnp.broadcast_to(head[r0:r0 + 1, :], (8, N)))
            ra = jnp.broadcast_to(a[t0][r0:r0 + 1, :], (8, N)) * inv
            rm = jnp.broadcast_to(m[t0][r0:r0 + 1, :], (8, N)) * inv
            f = jnp.where(sub > r0, head * inv, 0.0)
            a[t0] = jnp.where(sub == r0, ra, a[t0] - f * ra)
            m[t0] = jnp.where(sub == r0, rm, m[t0] - f * rm)
            for t in range(t0 + 1, last):
                f = jnp.broadcast_to(a[t][:, k:k + 1], (8, N)) * inv
                a[t] = a[t] - f * ra
                m[t] = m[t] - f * rm
        if last < T:
            pa = jnp.concatenate(a[p * B // 8:last], axis=0)
            pm = jnp.concatenate(m[p * B // 8:last], axis=0)
            lower = pa.T[(p + 1) * B:, :]
            change = exact(lower, jnp.concatenate([pa, pm], axis=1))
            for t in range(last, T):
                part = change[8 * (t - last):8 * (t - last) + 8]
                a[t] = a[t] - part[:, :N]
                m[t] = m[t] - part[:, N:]
    return jnp.concatenate(m, axis=0)


def finish_kernel(S, total, f, af, g, basis, image, projected):
    W = N // S
    gram = jnp.concatenate([g[t, 0:W] for t in range(S)], axis=0) * (1.0 / total)
    h_t = jnp.concatenate([g[t, W:2 * W] for t in range(S)], axis=0) * (1.0 / total)
    inv = inverse_factor(gram)
    projected[...] = exact(exact(inv, h_t, NT), inv, NT)
    mt = split(inv.T)

    def out(i, _):
        at = pl.ds(pl.multiple_of(i * N, N), N)
        fi = jnp.concatenate([f[t, i] for t in range(S)], axis=0).T
        basis[at, :] = mm3(split(fi), mt)
        ai = jnp.concatenate([af[t, i] for t in range(S)], axis=0).T
        image[at, :] = mm3(split(ai), mt)
        return 0

    lax.fori_loop(0, BD, out, 0)


def solution(mesh):
    S, R = mesh.shape["shift"], mesh.shape["rows"]
    Z = 8 if R % 32 == 0 else max(R // 2, 1)
    Y = R // Z
    W = N // S
    X = S // 2
    angle = np.pi * (np.repeat(np.arange(S), W) + 0.5) / S
    table = np.zeros((8, N), np.float32)
    table[0] = RADIUS * np.cos(angle)
    table[1] = RADIUS * np.sin(angle)
    table[2] = table[0] / S
    table[3] = table[1] / S
    dma = pltpu.SemaphoreType.DMA
    vmem = pltpu.VMEM
    any_spec = pl.BlockSpec(memory_space=pl.ANY)
    vm = pl.BlockSpec(memory_space=vmem)
    stack = jax.ShapeDtypeStruct((S, BD, W, N), F32)

    def per_device(neighbours, couplings, eigvectors, eigvalues, start_block):
        f, af, g = pl.pallas_call(
            functools.partial(main_kernel, S, R, Z),
            out_shape=(stack, stack, jax.ShapeDtypeStruct((S, 2 * W, N), F32)),
            in_specs=[pl.BlockSpec(memory_space=pltpu.SMEM)] + [any_spec] * 4 + [vm],
            out_specs=(any_spec, any_spec, any_spec),
            scratch_shapes=[
                vmem((BD, BD, N, N), F32),
                vmem((BD, 2 * N, BD * N), BF16),
                vmem((3 * BD, N, N), F32),
                vmem((3, BD, N), F32),
                vmem((BD * N, N), F32),
                vmem((3 * BD, W, N), F32),
                vmem((2, BD, N, N), BF16),
                vmem((2, BD, N, N), BF16),
                vmem((3 * BD, N, 2 * N), BF16),
                vmem((3 * BD, N, 2 * N), BF16),
                vmem((3 * BD, N, 2 * N), F32),
                vmem((3 * BD, N, 2 * N), BF16),
                vmem((3 * BD, N, 2 * N), BF16),
                vmem((BD, N, 2 * N), F32),
                vmem((BD, N, N), F32),
                vmem((BD, N, N), F32),
                vmem((BD, N, N), F32),
                vmem((3 * BD, W, N), F32),
                vmem((BD, W, N), F32),
                vmem((S, BD, W, N), F32),
                vmem((BD, W, N), F32),
                vmem((S, BD, W, N), F32),
                vmem((Z, 2 * W, N), F32),
                vmem((Y, 2 * W, N), F32),
                vmem((S, 2 * W, N), F32),
                dma, dma, dma, dma, dma((3,)),
                dma((2,)), dma((2,)), dma((2,)), dma((2,)),
                dma((2,)), dma((2,)), dma((2,)), dma((2,)),
                dma((2, BD)), dma((2, BD)), dma((2,)), dma((2,)),
                dma((X,)), dma((X,)), dma((X,)), dma((X,)),
                dma((X,)), dma((X,)), dma((X,)), dma((X,)),
                dma((Z,)), dma((Z,)), dma((Y,)), dma((Y,)), dma((S,)), dma((S,)),
            ],
            compiler_params=pltpu.CompilerParams(
                collective_id=0, has_side_effects=True
            ),
            name="filter",
        )(neighbours, couplings, eigvectors, eigvalues, start_block, jnp.asarray(table))
        rows_here = start_block.shape[0]
        return pl.pallas_call(
            functools.partial(finish_kernel, S, rows_here * R),
            out_shape=(
                jax.ShapeDtypeStruct((rows_here, N), F32),
                jax.ShapeDtypeStruct((rows_here, N), F32),
                jax.ShapeDtypeStruct((N, N), F32),
            ),
            in_specs=[vm, vm, vm],
            out_specs=(vm, vm, vm),
            name="finish",
        )(f, af, g)

    in_specs = (
        P("rows", None),
        P("rows", None, None, None),
        P("rows", None, None),
        P("rows", None),
        P("rows", None),
    )
    out_specs = (P("rows", None), P("rows", None), P())
    return jax.shard_map(
        per_device, mesh=mesh, in_specs=in_specs, out_specs=out_specs, check_vma=False
    )
```

```python
import functools

import jax
import jax.numpy as jnp
import numpy as np
from jax import lax
from jax.experimental import pallas as pl
from jax.experimental.pallas import tpu as pltpu
from jax.sharding import PartitionSpec as P

MESH = pl.DeviceIdType.MESH
F32 = jnp.float32
BF16 = jnp.bfloat16
BD = 8
N = 128
NN = ((1,), (0,))
NT = ((1,), (1,))
RADIUS = 1.0
DAMPING = 0.8


def split(x):
    hi = x.astype(BF16)
    return hi, (x - hi.astype(F32)).astype(BF16)


def mm(a, b, dims=NN):
    return lax.dot_general(a, b, (dims, ((), ())), preferred_element_type=F32)


def mm3(a, b, dims=NN):
    return mm(a[0], b[0], dims) + (mm(a[0], b[1], dims) + mm(a[1], b[0], dims))


def exact(a, b, dims=NN):
    return lax.dot_general(
        a, b, (dims, ((), ())), precision=lax.Precision.HIGHEST, preferred_element_type=F32
    )


def main_kernel(
    S, R, Z,
    nbr, c_hbm, q_hbm, e_hbm, b_hbm, consts,
    f_out, af_out, g_out,
    cv, c2s, qp, ep, bv, bp, qs, qt, xh, xl, x2, xh2, xl2, y2, dr, di, bt, ft, fh, fa, afs, afa,
    fu, au, zb, yb, gb,
    csem, qsem, esem, bsem, osem,
    q_s, q_r, qf_s, qf_r, e_s, e_r, b_s, b_r, x_s, x_r, f_s, f_r,
    ga_s, ga_r, gp_s, gp_r, ha_s, ha_r, hp_s, hp_r,
    z_s, z_r, y_s, y_r, g_s, g_r,
):
    W = N // S
    s = lax.axis_index("shift")
    r = lax.axis_index("rows")
    Y = R // Z
    yy, zz = r // Z, r % Z
    core = s % 2
    partner = s + 1 - 2 * core
    up, down = (r + 1) % R, (r + R - 1) % R
    X = S // 2
    xx = s // 2

    load_q = pltpu.make_async_copy(q_hbm, qp.at[pl.ds(BD, BD)], qsem)
    load_q.start()
    load_b = pltpu.make_async_copy(b_hbm, bv, bsem)
    load_b.start()
    load_e = pltpu.make_async_copy(e_hbm, ep.at[1], esem)
    load_e.start()
    load_c = pltpu.make_async_copy(c_hbm, cv, csem)
    load_c.start()

    barrier = pltpu.get_barrier_semaphore()

    def greet(where):
        pl.semaphore_signal(barrier, inc=1, device_id=where, device_id_type=MESH)

    greet({"rows": up})
    greet({"rows": down})
    for k in range(1, Z):
        greet({"rows": yy * Z + (zz + k) % Z})
    for k in range(1, Y):
        greet({"rows": ((yy + k) % Y) * Z + zz})
    for k in range(1, S):
        greet({"shift": (s + k) % S})

    def remote(src, dst, ss, rs, where):
        return pltpu.make_async_remote_copy(
            src_ref=src, dst_ref=dst, send_sem=ss, recv_sem=rs,
            device_id=where, device_id_type=MESH,
        )

    HB = BD // 2

    def q_copies(i):
        at = core * HB + i
        return (
            remote(q_hbm.at[at], qp.at[at], q_s.at[0, i], q_r.at[0, i], {"rows": up}),
            remote(q_hbm.at[at], qp.at[2 * BD + at], q_s.at[1, i], q_r.at[1, i], {"rows": down}),
        )

    def q_forward(i):
        at = core * HB + i
        return (
            remote(qp.at[at], qp.at[at], qf_s.at[0, i], qf_r.at[0, i], {"shift": partner}),
            remote(qp.at[2 * BD + at], qp.at[2 * BD + at], qf_s.at[1, i], qf_r.at[1, i],
                   {"shift": partner}),
        )

    e_up = remote(e_hbm, ep.at[0], e_s.at[0], e_r.at[0], {"rows": up})
    e_dn = remote(e_hbm, ep.at[2], e_s.at[1], e_r.at[1], {"rows": down})

    lane = lax.broadcasted_iota(jnp.int32, (W, N), 1)
    row = lax.broadcasted_iota(jnp.int32, (W, N), 0)
    pick = (lane == row + s * W).astype(BF16)

    load_q.wait()
    load_b.wait()
    load_e.wait()

    def own_rhs(i, _):
        q = qp[BD + i]
        qh, ql = split(q)
        qs[0, i] = qh
        qs[1, i] = ql
        th, tl = split(q.T)
        qt[0, i] = th
        qt[1, i] = tl
        blk = bv[pl.ds(pl.multiple_of(i * N, N), N), :]
        bh = blk.astype(BF16)
        rest = blk - bh.astype(F32)
        bl = rest.astype(BF16)
        bm = (rest - bl.astype(F32)).astype(BF16)
        own = mm(pick, bh, NT) + (mm(pick, bl, NT) + mm(pick, bm, NT))
        bp[BD + i] = mm3(split(own), (qh, ql))
        return 0

    lax.fori_loop(0, BD, own_rhs, 0, unroll=4)
    pl.semaphore_wait(barrier, 2 + (Z - 1) + (Y - 1) + (S - 1))
    e_up.start()
    e_dn.start()

    b_up = remote(bp.at[pl.ds(BD, BD)], bp.at[pl.ds(0, BD)], b_s.at[0], b_r.at[0], {"rows": up})
    b_dn = remote(bp.at[pl.ds(BD, BD)], bp.at[pl.ds(2 * BD, BD)], b_s.at[1], b_r.at[1], {"rows": down})
    b_up.start()
    b_dn.start()

    def q_send(i, _):
        for c in q_copies(i):
            c.start()
        return 0

    lax.fori_loop(0, HB, q_send, 0)

    za = consts[0:1, :]
    zbm = consts[1:2, :]
    wr = consts[2:3, :]
    wi = consts[3:4, :]

    def coefficients(e_row):
        offset = za - jnp.broadcast_to(e_row, (N, N)).T
        scale = DAMPING / (offset * offset + zbm * zbm)
        return offset * scale, -zbm * scale

    def spread(rhs):
        return jnp.concatenate([rhs] * S, axis=0).T

    def first(g, slot, qpair):
        c_re, c_im = coefficients(g)
        tile = spread(bp[slot])
        mixed = jnp.concatenate([c_re * tile, c_im * tile], axis=1)
        xv = mm3(qpair, split(mixed))
        h, l = split(xv)
        xh[slot] = h
        xl[slot] = l
        return c_re, c_im, tile, mixed

    def own_first(i, _):
        c_re, c_im, tile, mixed = first(ep[1, pl.ds(i, 1), :], BD + i, (qs[0, i], qs[1, i]))
        dr[i] = c_re
        di[i] = c_im
        bt[i] = tile
        y2[i] = mixed
        return 0

    lax.fori_loop(0, BD, own_first, 0, unroll=2)

    load_c.wait()

    def split_c(i, _):
        for k in range(BD):
            h, l = split(cv[i, k])
            c2s[i, 0:N, k * N:(k + 1) * N] = h
            c2s[i, N:2 * N, k * N:(k + 1) * N] = l
        return 0

    lax.fori_loop(0, BD, split_c, 0)

    e_up.wait_recv()
    e_dn.wait_recv()
    b_up.wait_recv()
    b_dn.wait_recv()

    def halo_first(i):
        first(ep[0, pl.ds(i, 1), :], i, split(qp[i]))
        first(ep[2, pl.ds(i, 1), :], 2 * BD + i, split(qp[2 * BD + i]))

    def direct(i, _):
        for c, on in zip(q_copies(i), q_forward(i)):
            c.wait_recv()
            on.start()
        halo_first(core * HB + i)
        return 0

    lax.fori_loop(0, HB, direct, 0)

    def forwarded(i, _):
        for on in q_forward(i):
            on.wait_recv()
        halo_first((1 - core) * HB + i)
        return 0

    lax.fori_loop(0, HB, forwarded, 0)

    base = r * BD - BD

    def place(i, k):
        return jnp.clip(nbr[i, k] - base, 0, 3 * BD - 1)

    def coupled(i, hi_ref, lo_ref):
        acc = jnp.zeros((N, 2 * N), F32)
        for k in range(0, BD, 2):
            i0 = place(i, k)
            i1 = place(i, k + 1)
            hi = jnp.concatenate([hi_ref[i0], hi_ref[i1]], axis=0)
            lo = jnp.concatenate([lo_ref[i0], lo_ref[i1]], axis=0)
            both = mm(c2s[i, :, k * N:(k + 2) * N], hi)
            acc = acc + both[:N] + both[N:] + mm(c2s[i, :N, k * N:(k + 2) * N], lo)
        return acc

    def relaxed(i, spun):
        t_re = bt[i] + spun[:, :N]
        t_im = spun[:, N:]
        c_re, c_im = dr[i], di[i]
        old = y2[i]
        return (
            (1.0 - DAMPING) * old[:, :N] + (c_re * t_re - c_im * t_im),
            (1.0 - DAMPING) * old[:, N:] + (c_re * t_im + c_im * t_re),
        )

    def x_copies(i):
        return (
            remote(x2.at[BD + i], x2.at[i], x_s.at[0, i], x_r.at[0, i], {"rows": up}),
            remote(x2.at[BD + i], x2.at[2 * BD + i], x_s.at[1, i], x_r.at[1, i], {"rows": down}),
        )

    def sweep_one(i, _):
        re, im = relaxed(i, mm3((qt[0, i], qt[1, i]), split(coupled(i, xh, xl))))
        mixed = jnp.concatenate([re, im], axis=1)
        y2[i] = mixed
        xv = mm3((qs[0, i], qs[1, i]), split(mixed))
        x2[BD + i] = xv
        to_up, to_dn = x_copies(i)
        to_up.start()
        to_dn.start()
        h, l = split(xv)
        xh2[BD + i] = h
        xl2[BD + i] = l
        return 0

    lax.fori_loop(0, BD, sweep_one, 0)

    def arrive(i, _):
        to_up, to_dn = x_copies(i)
        to_up.wait_recv()
        h, l = split(x2[i])
        xh2[i] = h
        xl2[i] = l
        to_dn.wait_recv()
        h, l = split(x2[2 * BD + i])
        xh2[2 * BD + i] = h
        xl2[2 * BD + i] = l
        return 0

    lax.fori_loop(0, BD, arrive, 0)

    def couple_two(i, _):
        h, l = split(coupled(i, xh2, xl2))
        xh[i] = h
        xl[i] = l
        return 0

    lax.fori_loop(0, BD, couple_two, 0, unroll=2)

    def sweep_two(i, _):
        re, im = relaxed(i, mm3((qt[0, i], qt[1, i]), (xh[i], xl[i])))
        t = (wr * re - wi * im).T
        hat = t[0:W]
        for j in range(1, S):
            hat = hat + t[j * W:(j + 1) * W]
        fh[i] = hat
        return 0

    lax.fori_loop(0, BD, sweep_two, 0, unroll=2)

    def filtered(i, _):
        hat = fh[i]
        q = (qs[0, i], qs[1, i])
        ft[BD + i] = mm3(split(hat), q, NT)
        afs[i] = mm3(split(hat * ep[1, pl.ds(i, 1), :]), q, NT)
        return 0

    lax.fori_loop(0, BD, filtered, 0, unroll=4)

    f_up = remote(ft.at[pl.ds(BD, BD)], ft.at[pl.ds(0, BD)], f_s.at[0], f_r.at[0], {"rows": up})
    f_dn = remote(ft.at[pl.ds(BD, BD)], ft.at[pl.ds(2 * BD, BD)], f_s.at[1], f_r.at[1], {"rows": down})
    f_up.start()
    f_dn.start()

    def gather_start(src, dst, ssem, rsem, psem, prsem):
        cross = []
        for k in range(1, X):
            c = remote(src, dst.at[s], ssem.at[k], rsem.at[k], {"shift": ((xx + k) % X) * 2 + core})
            c.start()
            cross.append(c)
        mine = remote(src, dst.at[s], psem.at[0], prsem.at[0], {"shift": partner})
        mine.start()
        return cross, mine

    def gather_forward(dst, cross, psem, prsem):
        on = []
        for k in range(1, X):
            cross[k - 1].wait_recv()
            origin = ((xx + X - k) % X) * 2 + core
            c = remote(dst.at[origin], dst.at[origin], psem.at[k], prsem.at[k], {"shift": partner})
            c.start()
            on.append(c)
        return on

    def gather_end(mine, on):
        mine.wait_recv()
        for c in on:
            c.wait_recv()

    f_cross, f_mine = gather_start(ft.at[pl.ds(BD, BD)], fa, ga_s, ga_r, gp_s, gp_r)
    fa[s] = ft[pl.ds(BD, BD)]
    f_up.wait_recv()
    f_dn.wait_recv()

    def image(i, _):
        acc = afs[i]
        for k in range(0, BD, 2):
            h, l = split(jnp.concatenate([ft[place(i, k)], ft[place(i, k + 1)]], axis=1))
            at = slice(k * N, (k + 2) * N)
            both = mm(jnp.concatenate([h, l], axis=0), c2s[i, :N, at], NT)
            acc = acc + (both[:W] + (both[W:] + mm(h, c2s[i, N:, at], NT)))
        afs[i] = acc
        return 0

    lax.fori_loop(0, BD, image, 0, unroll=2)

    f_on = gather_forward(fa, f_cross, gp_s, gp_r)
    h_cross, h_mine = gather_start(afs, afa, ha_s, ha_r, hp_s, hp_r)
    afa[s] = afs[...]
    gather_end(f_mine, f_on)

    def upright(i, dst, stack):
        h, l = split(jnp.concatenate([stack[t, i] for t in range(S)], axis=0).T)
        both = jnp.concatenate([h, l], axis=1)
        dst[pl.ds(pl.multiple_of(i * N, N), N), :] = both
        return both

    def grams(i, acc):
        both = upright(i, fu, fa)
        h, l = split(jnp.concatenate([ft[BD + i], afs[i]], axis=0))
        wide = mm(h, both)
        return acc + (wide[:, :N] + (wide[:, N:] + mm(l, both[:, :N])))

    zb[zz] = lax.fori_loop(0, BD, grams, jnp.zeros((2 * W, N), F32), unroll=4)

    z_cp = []
    for k in range(1, Z):
        c = remote(zb.at[zz], zb.at[zz], z_s.at[k], z_r.at[k], {"rows": yy * Z + (zz + k) % Z})
        c.start()
        z_cp.append(c)
    out_f = pltpu.make_async_copy(fu, f_out, osem.at[0])
    out_f.start()
    h_on = gather_forward(afa, h_cross, hp_s, hp_r)
    for c in z_cp:
        c.wait_recv()
    yb[yy] = functools.reduce(lambda a, t: a + zb[t], range(1, Z), zb[0])
    y_cp = []
    for k in range(1, Y):
        c = remote(yb.at[yy], yb.at[yy], y_s.at[k], y_r.at[k], {"rows": ((yy + k) % Y) * Z + zz})
        c.start()
        y_cp.append(c)
    for c in y_cp:
        c.wait_recv()
    gb[s] = functools.reduce(lambda a, t: a + yb[t], range(1, Y), yb[0])
    g_cp = []
    for k in range(1, S):
        c = remote(gb.at[s], gb.at[s], g_s.at[k], g_r.at[k], {"shift": (s + k) % S})
        c.start()
        g_cp.append(c)
    gather_end(h_mine, h_on)

    def af_upright(i, _):
        upright(i, au, afa)
        return 0

    lax.fori_loop(0, BD, af_upright, 0, unroll=2)
    out_h = pltpu.make_async_copy(au, af_out, osem.at[1])
    out_h.start()
    for c in g_cp:
        c.wait_recv()
    out_g = pltpu.make_async_copy(gb, g_out, osem.at[2])
    out_g.start()

    for c in (e_up, e_dn, b_up, b_dn, f_up, f_dn):
        c.wait_send()
    for c in f_cross + [f_mine] + f_on + h_cross + [h_mine] + h_on + z_cp + y_cp + g_cp:
        c.wait_send()

    def sent(i, _):
        to_up, to_dn = x_copies(i)
        to_up.wait_send()
        to_dn.wait_send()
        return 0

    lax.fori_loop(0, BD, sent, 0)

    def q_sent(i, _):
        for c in q_copies(i) + q_forward(i):
            c.wait_send()
        return 0

    lax.fori_loop(0, HB, q_sent, 0)
    out_f.wait()
    out_h.wait()
    out_g.wait()


def inverse_factor(g):
    T = N // 8
    sub = lax.broadcasted_iota(jnp.int32, (8, N), 0)
    lane = lax.broadcasted_iota(jnp.int32, (8, N), 1)
    a = [g[8 * t:8 * t + 8] for t in range(T)]
    m = [(lane == sub + 8 * t).astype(F32) for t in range(T)]

    def full(x):
        return jnp.broadcast_to(x, (8, N))

    for t in range(T):
        col = [full(a[t][:, 8 * t + j:8 * t + j + 1]) for j in range(8)]
        e = {(i, j): full(col[j][i:i + 1, :]) for j in range(8) for i in range(j, 8)}
        inv, low, ra, rm = [], {}, [], []
        for k in range(8):
            inv.append(lax.rsqrt(e[k, k]))
            for i in range(k + 1, 8):
                low[i, k] = e[i, k] * inv[k]
            for j in range(k + 1, 8):
                for i in range(j, 8):
                    e[i, j] = e[i, j] - low[i, k] * low[j, k]
            xa, xm = full(a[t][k:k + 1, :]), full(m[t][k:k + 1, :])
            for j in range(k):
                xa = xa - low[k, j] * ra[j]
                xm = xm - low[k, j] * rm[j]
            ra.append(xa * inv[k])
            rm.append(xm * inv[k])
        x = rm[0]
        for k in range(1, 8):
            x = jnp.where(sub == k, rm[k], x)
        m[t] = x
        for u in range(t + 1, T):
            ls = []
            for k in range(8):
                y = full(a[u][:, 8 * t + k:8 * t + k + 1])
                for j in range(k):
                    y = y - ls[j] * low[k, j]
                ls.append(y * inv[k])
            for k in range(8):
                a[u] = a[u] - ls[k] * ra[k]
                m[u] = m[u] - ls[k] * rm[k]
    return jnp.concatenate(m, axis=0)


def finish_kernel(S, total, f_hbm, af_hbm, g, basis, image, projected, fv, av, bv, iv, sem, osem):
    W = N // S
    load_f = pltpu.make_async_copy(f_hbm, fv, sem.at[0])
    load_f.start()
    load_a = pltpu.make_async_copy(af_hbm, av, sem.at[1])
    load_a.start()
    gram = jnp.concatenate([g[t, 0:W] for t in range(S)], axis=0) * (1.0 / total)
    h_t = jnp.concatenate([g[t, W:2 * W] for t in range(S)], axis=0) * (1.0 / total)
    inv = inverse_factor(gram)
    mh, ml = split(inv.T)
    twice = jnp.concatenate([mh, mh], axis=0)
    load_f.wait()
    load_a.wait()

    def stores(i):
        at = pl.ds(pl.multiple_of(i * N, N), N)
        return (
            pltpu.make_async_copy(bv.at[at, :], basis.at[at, :], osem.at[0, i]),
            pltpu.make_async_copy(iv.at[at, :], image.at[at, :], osem.at[1, i]),
        )

    def out(i, _):
        at = pl.ds(pl.multiple_of(i * N, N), N)
        fi = fv[at, :]
        bv[at, :] = mm(fi, twice) + mm(fi[:, :N], ml)
        ai = av[at, :]
        iv[at, :] = mm(ai, twice) + mm(ai[:, :N], ml)
        for c in stores(i):
            c.start()
        return 0

    lax.fori_loop(0, BD, out, 0, unroll=4)
    projected[...] = mm3(split(mm3(split(inv), split(h_t), NT)), (mh, ml))
    for i in range(BD):
        for c in stores(i):
            c.wait()


def solution(mesh):
    S, R = mesh.shape["shift"], mesh.shape["rows"]
    Z = 8 if R % 32 == 0 else max(R // 2, 1)
    Y = R // Z
    W = N // S
    X = S // 2
    angle = np.pi * (np.repeat(np.arange(S), W) + 0.5) / S
    table = np.zeros((8, N), np.float32)
    table[0] = RADIUS * np.cos(angle)
    table[1] = RADIUS * np.sin(angle)
    table[2] = table[0] / S
    table[3] = table[1] / S
    dma = pltpu.SemaphoreType.DMA
    vmem = pltpu.VMEM
    any_spec = pl.BlockSpec(memory_space=pl.ANY)
    vm = pl.BlockSpec(memory_space=vmem)
    stack = jax.ShapeDtypeStruct((BD * N, 2 * N), BF16)

    def per_device(neighbours, couplings, eigvectors, eigvalues, start_block):
        f, af, g = pl.pallas_call(
            functools.partial(main_kernel, S, R, Z),
            out_shape=(stack, stack, jax.ShapeDtypeStruct((S, 2 * W, N), F32)),
            in_specs=[pl.BlockSpec(memory_space=pltpu.SMEM)] + [any_spec] * 4 + [vm],
            out_specs=(any_spec, any_spec, any_spec),
            scratch_shapes=[
                vmem((BD, BD, N, N), F32),
                vmem((BD, 2 * N, BD * N), BF16),
                vmem((3 * BD, N, N), F32),
                vmem((3, BD, N), F32),
                vmem((BD * N, N), F32),
                vmem((3 * BD, W, N), F32),
                vmem((2, BD, N, N), BF16),
                vmem((2, BD, N, N), BF16),
                vmem((3 * BD, N, 2 * N), BF16),
                vmem((3 * BD, N, 2 * N), BF16),
                vmem((3 * BD, N, 2 * N), F32),
                vmem((3 * BD, N, 2 * N), BF16),
                vmem((3 * BD, N, 2 * N), BF16),
                vmem((BD, N, 2 * N), F32),
                vmem((BD, N, N), F32),
                vmem((BD, N, N), F32),
                vmem((BD, N, N), F32),
                vmem((3 * BD, W, N), F32),
                vmem((BD, W, N), F32),
                vmem((S, BD, W, N), F32),
                vmem((BD, W, N), F32),
                vmem((S, BD, W, N), F32),
                vmem((BD * N, 2 * N), BF16),
                vmem((BD * N, 2 * N), BF16),
                vmem((Z, 2 * W, N), F32),
                vmem((Y, 2 * W, N), F32),
                vmem((S, 2 * W, N), F32),
                dma, dma, dma, dma, dma((3,)),
                dma((2, BD // 2)), dma((2, BD // 2)), dma((2, BD // 2)), dma((2, BD // 2)),
                dma((2,)), dma((2,)), dma((2,)), dma((2,)),
                dma((2, BD)), dma((2, BD)), dma((2,)), dma((2,)),
                dma((X,)), dma((X,)), dma((X,)), dma((X,)),
                dma((X,)), dma((X,)), dma((X,)), dma((X,)),
                dma((Z,)), dma((Z,)), dma((Y,)), dma((Y,)), dma((S,)), dma((S,)),
            ],
            compiler_params=pltpu.CompilerParams(
                collective_id=0, has_side_effects=True
            ),
            name="filter",
        )(neighbours, couplings, eigvectors, eigvalues, start_block, jnp.asarray(table))
        rows_here = start_block.shape[0]
        return pl.pallas_call(
            functools.partial(finish_kernel, S, rows_here * R),
            out_shape=(
                jax.ShapeDtypeStruct((rows_here, N), F32),
                jax.ShapeDtypeStruct((rows_here, N), F32),
                jax.ShapeDtypeStruct((N, N), F32),
            ),
            in_specs=[any_spec, any_spec, vm],
            out_specs=(any_spec, any_spec, vm),
            scratch_shapes=[
                vmem((BD * N, 2 * N), BF16),
                vmem((BD * N, 2 * N), BF16),
                vmem((BD * N, N), F32),
                vmem((BD * N, N), F32),
                dma((2,)),
                dma((2, BD)),
            ],
            name="finish",
        )(f, af, g)

    in_specs = (
        P("rows", None),
        P("rows", None, None, None),
        P("rows", None, None),
        P("rows", None),
        P("rows", None),
    )
    out_specs = (P("rows", None), P("rows", None), P())
    return jax.shard_map(
        per_device, mesh=mesh, in_specs=in_specs, out_specs=out_specs, check_vma=False
    )
```
